32 devices in a mesh: seq: 8 (over y, x, core), batch: 4 (over z).
Axes of the slice: x: 2, y: 2, z: 4, core: 2. Of those that a mesh axis runs over, the one named last changes fastest.
Arguments:
- queries: bfloat16 [16, 4096], P('batch', 'seq'), may hold values from -210 to 210
- key_cache: bfloat16 [16, 1024, 2048], P('batch', 'seq'), may hold values from -6 to 6
- value_cache: bfloat16 [16, 1024, 2048], P('batch', 'seq'), may hold values from -12 to 12
- new_key: bfloat16 [16, 2048], P('batch'), may hold values from -6 to 6
- new_value: bfloat16 [16, 2048], P('batch'), may hold values from -12 to 12
- page_table: int32 [16, 8], P('batch', 'seq'), may hold values from 0 to 3, as said below
- counts: int32 [16, 8], P('batch', 'seq'), may hold values from 1 to 128
- offsets: int32 [16], P('batch'), may hold values from 0 to 896
- w_out: bfloat16 [4096, 4608], P('seq', 'batch'), may hold values from -0.09375 to 0.09375
Outputs:
- projected: bfloat16 [16, 4608], P('seq', 'batch')
The draws below stay inside these ranges and needn't reach their ends.
Inputs may be any that keep to these rules, and one draw needn't show every extreme that they name: `page_table`: for each group of 4 requests and each index along seq, the slots of that index's 1 pages of the group's requests are all different.
All inputs are finite; a program needn't handle non-finite values.
Results may differ from the reference program's by a relative error of at most 0.005.
Values may be sent and summed in bfloat16 or wider, within the bound.
A program may use at most 64 MiB of HBM per device.

```python
import jax
import jax.numpy as jnp
from jax import lax

D = 4608
HEADS = 32
KVH = 16
HD = 128
QSCALAR = 144
PAGE = 128
REQ_DEV = 4
PAGES_DEV = 1
BATCH = 16
SLOTS = 4
NPAGES = 8
N_SEQ = 8
N_BATCH = 4


def slot_table(key):
    subkeys = jax.random.split(jax.random.fold_in(key, 11), N_BATCH * N_SEQ)
    orders = jax.vmap(lambda subkey: jax.random.permutation(subkey, SLOTS))(subkeys)
    orders = orders.reshape(N_BATCH, N_SEQ, REQ_DEV, PAGES_DEV).transpose(0, 2, 1, 3)
    return orders.reshape(N_BATCH * REQ_DEV, N_SEQ * PAGES_DEV).astype(jnp.int32)


def draw_page_table(key, part):
    return slot_table(key)


def draw_queries(key, part):
    drawn = 3.0 * jnp.clip(jax.random.normal(jax.random.fold_in(key, 31), (BATCH, HEADS, HD), jnp.float32), -6.0, 6.0)
    return drawn.reshape(BATCH, HEADS * HD).astype(jnp.bfloat16)


def draw_key_cache(key, part):
    key_values = jnp.clip(jax.random.normal(jax.random.fold_in(key, 41), (N_BATCH * SLOTS, N_SEQ * PAGE, KVH * HD), jnp.float32), -6.0, 6.0)
    return key_values.astype(jnp.bfloat16)


def draw_new_key(key, part):
    fresh_keys = jnp.clip(jax.random.normal(jax.random.fold_in(key, 53), (BATCH, KVH * HD), jnp.float32), -6.0, 6.0)
    return fresh_keys.astype(jnp.bfloat16)


def place_ends(result, key, low, top_value):
    place = [jax.random.randint(jax.random.fold_in(key, axis), (), 0, length) for axis, length in enumerate(result.shape)]
    longest = result.shape.index(max(result.shape))
    beside = place[:longest] + [(place[longest] + 1) % result.shape[longest]] + place[longest + 1:]
    return result.at[tuple(place)].set(low).at[tuple(beside)].set(top_value)


def shard_levels(rng, dims, cuts, smallest, top_value):
    level = 1.0
    for axis_at, parts in cuts:
        draws = jax.random.uniform(jax.random.fold_in(jax.random.fold_in(rng, 6), axis_at), (parts,), jnp.float32, smallest / len(cuts), top_value / len(cuts))
        level = level * jnp.repeat(jnp.exp(draws), dims[axis_at] // parts).reshape((-1,) + (1,) * (len(dims) - 1 - axis_at))
    return level


def noise(key, shape, deviation, most, pieces=(), kind=jnp.bfloat16):
    values = deviation * jax.random.normal(key, shape, jnp.float32)
    if pieces:
        values = values * shard_levels(key, shape, pieces, -0.22, 0.18)
    return jnp.clip(values, -most, most).astype(kind)


def setup_inputs(seed: int = 0) -> dict:
    arg_keys = jax.random.split(jax.random.key(seed), 10)
    queries = draw_queries(jax.random.fold_in(arg_keys[9], 71), 0)
    key_cache = draw_key_cache(jax.random.fold_in(arg_keys[9], 71), 0)
    value_cache = noise(arg_keys[2], (SLOTS * N_BATCH, PAGE * N_SEQ, KVH * HD), 2.0, 12.0, ((0, 4), (1, 8)))
    new_key = draw_new_key(jax.random.fold_in(arg_keys[9], 71), 0)
    new_value = noise(arg_keys[4], (BATCH, KVH * HD), 2.0, 12.0, ((0, 4),))
    page_table = draw_page_table(jax.random.fold_in(arg_keys[9], 71), 0)
    counts = place_ends(jax.random.randint(arg_keys[6], (BATCH, NPAGES), 1, PAGE + 1), jax.random.fold_in(arg_keys[6], 1), 1, PAGE).astype(jnp.int32)
    offsets = place_ends(jax.random.randint(arg_keys[7], (BATCH,), 0, NPAGES * PAGE - PAGE + 1), jax.random.fold_in(arg_keys[7], 1), 0, NPAGES * PAGE - PAGE).astype(jnp.int32)
    w_out = noise(arg_keys[8], (HEADS * HD, D), (HEADS * HD) ** -0.5, 0.09375, ((0, 8), (1, 4)))
    return dict(queries=queries, key_cache=key_cache, value_cache=value_cache, new_key=new_key, new_value=new_value, page_table=page_table, counts=counts, offsets=offsets, w_out=w_out)


floor_score = -1.0e30


def reference(queries, key_cache, value_cache, new_key, new_value, page_table, counts, offsets, w_out):
    groups = HEADS // KVH
    score_multiplier = QSCALAR ** -0.5
    query_lattice = queries.astype(jnp.float32).reshape(BATCH, KVH, groups, HD)
    owner_row = (jnp.arange(BATCH, dtype=jnp.int32) // REQ_DEV) * SLOTS
    token_index = jnp.arange(PAGE, dtype=jnp.int32)

    def page_block(column_tile_block):
        key_slab = lax.dynamic_slice_in_dim(key_cache, column_tile_block * PAGE, PAGE, 1)
        value_slab = lax.dynamic_slice_in_dim(value_cache, column_tile_block * PAGE, PAGE, 1)
        slot_cols = lax.dynamic_slice_in_dim(page_table, column_tile_block * PAGES_DEV, PAGES_DEV, 1)
        live_counts = lax.dynamic_slice_in_dim(counts, column_tile_block * PAGES_DEV, PAGES_DEV, 1)
        slot_rows = owner_row[:, None] + slot_cols
        key_rows = key_slab[slot_rows].astype(jnp.float32).reshape(BATCH, PAGES_DEV * PAGE, KVH, HD)
        value_rows = value_slab[slot_rows].astype(jnp.float32).reshape(BATCH, PAGES_DEV * PAGE, KVH, HD)
        page_start = (column_tile_block * PAGES_DEV + jnp.arange(PAGES_DEV, dtype=jnp.int32)) * PAGE
        live_mask = (token_index[None, None, :] < live_counts[:, :, None]) & (
            page_start[None, :, None] + token_index[None, None, :] >= offsets[:, None, None])
        live_mask = live_mask.reshape(BATCH, PAGES_DEV * PAGE)[:, None, None, :]
        scores = jnp.einsum("bkgd,btkd->bkgt", query_lattice, key_rows) * score_multiplier
        peak_score = jnp.max(jnp.where(live_mask, scores, floor_score), axis=-1)
        weights = jnp.where(live_mask, jnp.exp(scores - peak_score[..., None]), 0.0)
        block_total = jnp.sum(weights, axis=-1)
        rounded = lax.optimization_barrier(weights.astype(jnp.bfloat16)).astype(jnp.float32)
        block_sum = jnp.einsum("bkgt,btkd->bkgd", rounded, value_rows)
        return peak_score, block_total, block_sum

    peaks, totals, sums = lax.map(page_block, jnp.arange(N_SEQ, dtype=jnp.int32))
    incoming_keys = new_key.astype(jnp.float32).reshape(BATCH, KVH, HD)
    incoming_score = jnp.einsum("pcoz,pcz->pco", query_lattice, incoming_keys) * score_multiplier
    top_score = jnp.maximum(jnp.max(peaks, axis=0), incoming_score)
    factor = jnp.exp(peaks - top_score[None])
    own_weight = jnp.exp(incoming_score - top_score)
    denominator = jnp.sum(totals * factor, axis=0) + own_weight
    fresh_value = new_value.astype(jnp.float32).reshape(BATCH, KVH, 1, HD)
    numerator = jnp.sum(sums * factor[..., None], axis=0) + own_weight[..., None] * fresh_value
    attention = (numerator / denominator[..., None]).astype(jnp.bfloat16).reshape(BATCH, HEADS * HD)
    return jnp.dot(attention, w_out, preferred_element_type=jnp.float32).astype(jnp.bfloat16)
```

```python
import functools

import jax
import jax.numpy as jnp
from jax import lax
from jax.experimental import pallas as pl
from jax.experimental.pallas import tpu as pltpu
from jax.sharding import PartitionSpec as P

HEADS = 32
KVH = 16
HD = 128
QSCALAR = 144
CHUNK = 2

floor_score = -1e30


def kernel(
    n,
    nb,
    q_hbm,
    k_hbm,
    v_hbm,
    nk_hbm,
    nv_hbm,
    table,
    counts,
    offsets,
    w_hbm,
    out_ref,
    q_all,
    k_ref,
    v_ref,
    nk_ref,
    nv_ref,
    w_ref,
    stat_send,
    stat_recv,
    sum_send,
    sum_recv,
    att_all,
    proj_send,
    proj_recv,
    load_sem,
    q_ss,
    q_rs,
    stat_ss,
    stat_rs,
    sum_ss,
    sum_rs,
    att_ss,
    att_rs,
    proj_ss,
    proj_rs,
):
    me = lax.axis_index("seq")
    mine = lax.axis_index("batch")
    requests = q_hbm.shape[0]
    slots, page_len, _ = k_hbm.shape
    pages = table.shape[1]
    tokens = slots * page_len
    groups = HEADS // KVH
    own = HEADS // n
    width = CHUNK * HD
    chunk_heads = CHUNK * groups
    rows = chunk_heads * requests
    n_chunks = KVH // CHUNK
    scale = QSCALAR ** (-0.5)
    f32 = jnp.float32

    loads = [
        pltpu.make_async_copy(src, dst, load_sem.at[i])
        for i, (src, dst) in enumerate(
            (
                (q_hbm, q_all.at[me]),
                (k_hbm, k_ref),
                (v_hbm, v_ref),
                (nk_hbm, nk_ref),
                (nv_hbm, nv_ref),
                (w_hbm, w_ref),
            )
        )
    ]
    for load in loads:
        load.start()

    barrier = pltpu.get_barrier_semaphore()
    for i in range(1, n):
        pl.semaphore_signal(barrier, inc=1, device_id={"seq": lax.rem(me + i, n)})
    for i in range(1, nb):
        pl.semaphore_signal(barrier, inc=1, device_id={"batch": lax.rem(mine + i, nb)})
    pl.semaphore_wait(barrier, n - 1 + nb - 1)

    def push(src, dst, ss, rs, axis, place, to):
        return pltpu.make_async_remote_copy(
            src_ref=src,
            dst_ref=dst,
            send_sem=ss.at[to],
            recv_sem=rs.at[place],
            device_id={axis: to},
        )

    for i in range(1, n):
        push(q_hbm, q_all.at[me], q_ss, q_rs, "seq", me, lax.rem(me + i, n)).start()

    row_request = lax.broadcasted_iota(jnp.int32, (rows, tokens), 0) % requests
    column = lax.broadcasted_iota(jnp.int32, (rows, tokens), 1)
    slot, token = column // page_len, column % page_len
    live = jnp.zeros((rows, tokens), jnp.bool_)
    first = jnp.zeros((rows, tokens), jnp.int32)
    for r in range(requests):
        first = jnp.where(row_request == r, offsets[r], first)
    for p in range(pages):
        where_at = jnp.zeros((rows, tokens), jnp.int32)
        count = jnp.zeros((rows, tokens), jnp.int32)
        for r in range(requests):
            where_at = jnp.where(row_request == r, table[r, p], where_at)
            count = jnp.where(row_request == r, counts[r, p], count)
        start = (me * pages + p) * page_len
        live = live | ((where_at == slot) & (token < count) & (start + token >= first))

    row = lax.broadcasted_iota(jnp.int32, (rows, HD), 0)
    lane = lax.broadcasted_iota(jnp.int32, (rows, HD), 1)

    def head_rows(ref, lead, head):
        at = pl.ds(pl.multiple_of(head * HD, HD), HD)
        return (ref[lead, :, at] if lead is not None else ref[:, at]).astype(f32)

    for load in loads[:3]:
        load.wait()
    for i in range(1, n):
        to = lax.rem(me + i, n)
        push(q_hbm, q_all.at[to], q_ss, q_rs, "seq", to, to).wait_recv()

    base = (me * own) // chunk_heads
    span = min(own, chunk_heads)
    for i in range(n_chunks):
        c = lax.rem(base + 1 + i, n_chunks)
        at = pl.ds(pl.multiple_of(c * width, width), width)
        head0 = c * chunk_heads
        parts = []
        for h in range(chunk_heads):
            parts.append(head_rows(q_all, (head0 + h) // own, (head0 + h) % own))
        q = jnp.concatenate(parts, axis=0)
        wide = jnp.concatenate(
            [
                jnp.where(row // (groups * requests) == k, q, 0.0).astype(jnp.bfloat16)
                for k in range(CHUNK)
            ],
            axis=1,
        )
        keys = k_ref[:, :, at].reshape(tokens, width)
        scores = (
            lax.dot_general(wide, keys, (((1,), (1,)), ((), ())), preferred_element_type=f32)
            * scale
        )
        peak = jnp.max(jnp.where(live, scores, floor_score), axis=1, keepdims=True)
        weights = jnp.where(live, jnp.exp(scores - peak), 0.0)
        total = jnp.sum(weights, axis=1, keepdims=True)
        values = v_ref[:, :, at].reshape(tokens, width)
        full = jnp.dot(weights.astype(jnp.bfloat16), values, preferred_element_type=f32)
        sums = jnp.concatenate(
            [
                full[k * groups * requests : (k + 1) * groups * requests, k * HD : (k + 1) * HD]
                for k in range(CHUNK)
            ],
            axis=0,
        )
        for part in range(chunk_heads // span):
            to = (head0 + part * span) // own
            height = span * requests
            low = part * height
            low_to = pl.multiple_of(((head0 + part * span) % own) * requests, requests)
            if own == span:
                low_to = 0
            hit = (row - low + low_to == lane) & (row >= low) & (row < low + height)
            stat = jnp.concatenate(
                [
                    jnp.sum(jnp.where(hit, peak, 0.0), axis=0, keepdims=True),
                    jnp.sum(jnp.where(hit, total, 0.0), axis=0, keepdims=True),
                ],
                axis=0,
            )
            stat_send[to] = stat
            sum_send[to] = sums[low : low + height].astype(sum_send.dtype)

            @pl.when(to != me)
            def _():
                push(stat_send.at[to], stat_recv.at[me], stat_ss, stat_rs, "seq", me, to).start()
                push(sum_send.at[to], sum_recv.at[me], sum_ss, sum_rs, "seq", me, to).start()

    own_rows = own * requests
    for load in loads[3:]:
        load.wait()
    kv = [(me * own + h) // groups for h in range(own)]
    own_q = jnp.concatenate([head_rows(q_all, me, h) for h in range(own)], axis=0)
    own_key = jnp.concatenate([head_rows(nk_ref, None, k) for k in kv], axis=0)
    own_value = jnp.concatenate([head_rows(nv_ref, None, k) for k in kv], axis=0)
    new_score = jnp.sum(own_q * own_key, axis=1, keepdims=True) * scale

    o_row = lax.broadcasted_iota(jnp.int32, (own_rows, HD), 0)
    o_lane = lax.broadcasted_iota(jnp.int32, (own_rows, HD), 1)
    diagonal = o_row == o_lane

    def to_column(line):
        return jnp.sum(jnp.where(diagonal, line, 0.0), axis=1, keepdims=True)

    for i in range(1, n):
        to = lax.rem(me + i, n)
        push(stat_send.at[to], stat_recv.at[to], stat_ss, stat_rs, "seq", to, to).wait_recv()
    stats = [stat_send[me]] + [stat_recv[lax.rem(me + i, n)] for i in range(1, n)]
    peaks = [to_column(s[0:1]) for s in stats]
    totals = [to_column(s[1:2]) for s in stats]
    top = new_score
    for peak in peaks:
        top = jnp.maximum(top, peak)
    own_weight = jnp.exp(new_score - top)
    factors = [jnp.exp(peak - top) for peak in peaks]
    denominator = own_weight
    for total, factor in zip(totals, factors):
        denominator = denominator + total * factor
    numerator = own_weight * own_value + factors[0] * sum_send[me].astype(f32)
    for i in range(1, n):
        to = lax.rem(me + i, n)
        push(sum_send.at[to], sum_recv.at[to], sum_ss, sum_rs, "seq", to, to).wait_recv()
        numerator = numerator + factors[i] * sum_recv[to].astype(f32)
    attention = numerator / denominator
    for h in range(own):
        att_all[mine, :, h * HD : (h + 1) * HD] = attention[
            h * requests : (h + 1) * requests
        ].astype(jnp.bfloat16)
    for i in range(1, nb):
        to = lax.rem(mine + i, nb)
        push(att_all.at[mine], att_all.at[mine], att_ss, att_rs, "batch", mine, to).start()
    for i in range(1, nb):
        to = lax.rem(mine + i, nb)
        push(att_all.at[mine], att_all.at[to], att_ss, att_rs, "batch", to, to).wait_recv()

    everyone = jnp.concatenate([att_all[b].astype(f32) for b in range(nb)], axis=0)
    projected = jnp.dot(everyone.astype(jnp.bfloat16), w_ref[...], preferred_element_type=f32)
    lines = out_ref.shape[0]
    for s in range(n):
        proj_send[s] = projected[s * lines : (s + 1) * lines].astype(proj_send.dtype)
    for i in range(1, n):
        to = lax.rem(me + i, n)
        push(proj_send.at[to], proj_recv.at[me], proj_ss, proj_rs, "seq", me, to).start()
    result = proj_send[me].astype(f32)
    for i in range(1, n):
        to = lax.rem(me + i, n)
        push(proj_send.at[to], proj_recv.at[to], proj_ss, proj_rs, "seq", to, to).wait_recv()
        result = result + proj_recv[to].astype(f32)
    out_ref[...] = result.astype(out_ref.dtype)

    for i in range(1, n):
        to = lax.rem(me + i, n)
        push(q_hbm, q_all.at[me], q_ss, q_rs, "seq", me, to).wait_send()
        push(stat_send.at[to], stat_recv.at[me], stat_ss, stat_rs, "seq", me, to).wait_send()
        push(sum_send.at[to], sum_recv.at[me], sum_ss, sum_rs, "seq", me, to).wait_send()
        push(proj_send.at[to], proj_recv.at[me], proj_ss, proj_rs, "seq", me, to).wait_send()
    for i in range(1, nb):
        to = lax.rem(mine + i, nb)
        push(att_all.at[mine], att_all.at[mine], att_ss, att_rs, "batch", mine, to).wait_send()


def on_device(n, nb, *args):
    queries, key_cache, value_cache, new_key, new_value, table, counts, offsets, w_out = args
    requests = queries.shape[0]
    own = HEADS // n
    lines = requests * nb // n
    columns = w_out.shape[1]
    bf16, f32 = jnp.bfloat16, jnp.float32
    hbm = pl.BlockSpec(memory_space=pl.ANY)
    smem = pl.BlockSpec(memory_space=pltpu.SMEM)
    dma = pltpu.SemaphoreType.DMA
    return pl.pallas_call(
        functools.partial(kernel, n, nb),
        out_shape=jax.ShapeDtypeStruct((lines, columns), bf16),
        in_specs=[hbm] * 5 + [smem] * 3 + [hbm],
        out_specs=pl.BlockSpec(memory_space=pltpu.VMEM),
        scratch_shapes=[
            pltpu.VMEM((n,) + queries.shape, bf16),
            pltpu.VMEM(key_cache.shape, bf16),
            pltpu.VMEM(value_cache.shape, bf16),
            pltpu.VMEM(new_key.shape, bf16),
            pltpu.VMEM(new_value.shape, bf16),
            pltpu.VMEM(w_out.shape, bf16),
            pltpu.VMEM((n, 2, HD), f32),
            pltpu.VMEM((n, 2, HD), f32),
            pltpu.VMEM((n, own * requests, HD), f32),
            pltpu.VMEM((n, own * requests, HD), f32),
            pltpu.VMEM((nb,) + queries.shape, bf16),
            pltpu.VMEM((n, lines, columns), f32),
            pltpu.VMEM((n, lines, columns), f32),
            dma((6,)),
            dma((n,)),
            dma((n,)),
            dma((n,)),
            dma((n,)),
            dma((n,)),
            dma((n,)),
            dma((nb,)),
            dma((nb,)),
            dma((n,)),
            dma((n,)),
        ],
        compiler_params=pltpu.CompilerParams(collective_id=0, has_side_effects=True),
    )(*args)


def solution(mesh):
    placed = (
        P("batch", "seq"),
        P("batch", "seq", None),
        P("batch", "seq", None),
        P("batch", None),
        P("batch", None),
        P("batch", "seq"),
        P("batch", "seq"),
        P("batch"),
        P("seq", "batch"),
    )
    return jax.shard_map(
        functools.partial(on_device, mesh.shape["seq"], mesh.shape["batch"]),
        mesh=mesh,
        in_specs=placed,
        out_specs=P("seq", "batch"),
        check_vma=False,
    )
```

```python
import functools

import jax
import jax.numpy as jnp
from jax import lax
from jax.experimental import pallas as pl
from jax.experimental.pallas import tpu as pltpu
from jax.sharding import PartitionSpec as P

HEADS = 32
KVH = 16
HD = 128
QSCALAR = 144
CHUNK = 2

floor_score = -1e30


def kernel(
    n,
    nb,
    q_hbm,
    k_hbm,
    v_hbm,
    nk_hbm,
    nv_hbm,
    table,
    counts,
    offsets,
    w_hbm,
    out_ref,
    q_all,
    k_ref,
    v_ref,
    nk_ref,
    nv_ref,
    w_ref,
    stat_send,
    stat_recv,
    sum_send,
    sum_recv,
    att_all,
    proj_send,
    proj_recv,
    load_sem,
    q_ss,
    q_rs,
    stat_ss,
    stat_rs,
    sum_ss,
    sum_rs,
    att_ss,
    att_rs,
    proj_ss,
    proj_rs,
):
    me = lax.axis_index("seq")
    mine = lax.axis_index("batch")
    requests = q_hbm.shape[0]
    slots, page_len, _ = k_hbm.shape
    pages = table.shape[0]
    tokens = slots * page_len
    groups = HEADS // KVH
    own = HEADS // n
    width = CHUNK * HD
    chunk_heads = CHUNK * groups
    rows = chunk_heads * requests
    n_chunks = KVH // CHUNK
    scale = QSCALAR ** (-0.5)
    f32 = jnp.float32

    loads = [
        pltpu.make_async_copy(src, dst, load_sem.at[i])
        for i, (src, dst) in enumerate(
            (
                (q_hbm, q_all.at[me]),
                (k_hbm, k_ref),
                (v_hbm, v_ref),
                (nk_hbm, nk_ref),
                (nv_hbm, nv_ref),
                (w_hbm, w_ref),
            )
        )
    ]
    for load in loads:
        load.start()

    barrier = pltpu.get_barrier_semaphore()
    for i in range(1, n):
        pl.semaphore_signal(barrier, inc=1, device_id={"seq": lax.rem(me + i, n)})
    for i in range(1, nb):
        pl.semaphore_signal(barrier, inc=1, device_id={"batch": lax.rem(mine + i, nb)})
    pl.semaphore_wait(barrier, n - 1 + nb - 1)

    def push(src, dst, ss, rs, axis, place, to):
        return pltpu.make_async_remote_copy(
            src_ref=src,
            dst_ref=dst,
            send_sem=ss.at[to],
            recv_sem=rs.at[place],
            device_id={axis: to},
        )

    for i in range(1, n):
        push(q_hbm, q_all.at[me], q_ss, q_rs, "seq", me, lax.rem(me + i, n)).start()

    row_request = lax.broadcasted_iota(jnp.int32, (rows, tokens), 0) % requests
    column = lax.broadcasted_iota(jnp.int32, (rows, tokens), 1)
    slot, token = column // page_len, column % page_len
    live = jnp.zeros((rows, tokens), jnp.bool_)
    first = jnp.zeros((rows, tokens), jnp.int32)
    for r in range(requests):
        first = jnp.where(row_request == r, offsets[r], first)
    for p in range(pages):
        where_at = jnp.zeros((rows, tokens), jnp.int32)
        count = jnp.zeros((rows, tokens), jnp.int32)
        for r in range(requests):
            where_at = jnp.where(row_request == r, table[p, r], where_at)
            count = jnp.where(row_request == r, counts[p, r], count)
        start = (me * pages + p) * page_len
        live = live | ((where_at == slot) & (token < count) & (start + token >= first))

    row = lax.broadcasted_iota(jnp.int32, (rows, HD), 0)
    lane = lax.broadcasted_iota(jnp.int32, (rows, HD), 1)

    def head_rows(ref, lead, head):
        at = pl.ds(pl.multiple_of(head * HD, HD), HD)
        return (ref[lead, :, at] if lead is not None else ref[:, at]).astype(f32)

    for load in loads[:3]:
        load.wait()
    for i in range(1, n):
        to = lax.rem(me + i, n)
        push(q_hbm, q_all.at[to], q_ss, q_rs, "seq", to, to).wait_recv()

    base = (me * own) // chunk_heads
    span = min(own, chunk_heads)
    for i in range(n_chunks):
        c = lax.rem(base + 1 + i, n_chunks)
        at = pl.ds(pl.multiple_of(c * width, width), width)
        head0 = c * chunk_heads
        parts = []
        for h in range(chunk_heads):
            parts.append(head_rows(q_all, (head0 + h) // own, (head0 + h) % own))
        q = jnp.concatenate(parts, axis=0)
        wide = jnp.concatenate(
            [
                jnp.where(row // (groups * requests) == k, q, 0.0).astype(jnp.bfloat16)
                for k in range(CHUNK)
            ],
            axis=1,
        )
        keys = k_ref[:, :, at].reshape(tokens, width)
        scores = (
            lax.dot_general(wide, keys, (((1,), (1,)), ((), ())), preferred_element_type=f32)
            * scale
        )
        peak = jnp.max(jnp.where(live, scores, floor_score), axis=1, keepdims=True)
        weights = jnp.where(live, jnp.exp(scores - peak), 0.0)
        total = jnp.sum(weights, axis=1, keepdims=True)
        values = v_ref[:, :, at].reshape(tokens, width)
        full = jnp.dot(weights.astype(jnp.bfloat16), values, preferred_element_type=f32)
        sums = jnp.concatenate(
            [
                full[k * groups * requests : (k + 1) * groups * requests, k * HD : (k + 1) * HD]
                for k in range(CHUNK)
            ],
            axis=0,
        )
        for part in range(chunk_heads // span):
            to = (head0 + part * span) // own
            height = span * requests
            low = part * height
            low_to = pl.multiple_of(((head0 + part * span) % own) * requests, requests)
            if own == span:
                low_to = 0
            hit = (row - low + low_to == lane) & (row >= low) & (row < low + height)
            stat = jnp.concatenate(
                [
                    jnp.sum(jnp.where(hit, peak, 0.0), axis=0, keepdims=True),
                    jnp.sum(jnp.where(hit, total, 0.0), axis=0, keepdims=True),
                ],
                axis=0,
            )
            stat_send[to] = stat
            sum_send[to] = sums[low : low + height].astype(sum_send.dtype)

            @pl.when(to != me)
            def _():
                push(stat_send.at[to], stat_recv.at[me], stat_ss, stat_rs, "seq", me, to).start()
                push(sum_send.at[to], sum_recv.at[me], sum_ss, sum_rs, "seq", me, to).start()

    own_rows = own * requests
    for load in loads[3:]:
        load.wait()
    kv = [(me * own + h) // groups for h in range(own)]
    own_q = jnp.concatenate([head_rows(q_all, me, h) for h in range(own)], axis=0)
    own_key = jnp.concatenate([head_rows(nk_ref, None, k) for k in kv], axis=0)
    own_value = jnp.concatenate([head_rows(nv_ref, None, k) for k in kv], axis=0)
    new_score = jnp.sum(own_q * own_key, axis=1, keepdims=True) * scale

    o_row = lax.broadcasted_iota(jnp.int32, (own_rows, HD), 0)
    o_lane = lax.broadcasted_iota(jnp.int32, (own_rows, HD), 1)
    diagonal = o_row == o_lane

    def to_column(line):
        return jnp.sum(jnp.where(diagonal, line, 0.0), axis=1, keepdims=True)

    for i in range(1, n):
        to = lax.rem(me + i, n)
        push(stat_send.at[to], stat_recv.at[to], stat_ss, stat_rs, "seq", to, to).wait_recv()
    stats = [stat_send[me]] + [stat_recv[lax.rem(me + i, n)] for i in range(1, n)]
    peaks = [to_column(s[0:1]) for s in stats]
    totals = [to_column(s[1:2]) for s in stats]
    top = new_score
    for peak in peaks:
        top = jnp.maximum(top, peak)
    own_weight = jnp.exp(new_score - top)
    factors = [jnp.exp(peak - top) for peak in peaks]
    denominator = own_weight
    for total, factor in zip(totals, factors):
        denominator = denominator + total * factor
    numerator = own_weight * own_value + factors[0] * sum_send[me].astype(f32)
    for i in range(1, n):
        to = lax.rem(me + i, n)
        push(sum_send.at[to], sum_recv.at[to], sum_ss, sum_rs, "seq", to, to).wait_recv()
        numerator = numerator + factors[i] * sum_recv[to].astype(f32)
    attention = numerator / denominator
    for h in range(own):
        att_all[mine, :, h * HD : (h + 1) * HD] = attention[
            h * requests : (h + 1) * requests
        ].astype(jnp.bfloat16)
    for i in range(1, nb):
        to = lax.rem(mine + i, nb)
        push(att_all.at[mine], att_all.at[mine], att_ss, att_rs, "batch", mine, to).start()
    for i in range(1, nb):
        to = lax.rem(mine + i, nb)
        push(att_all.at[mine], att_all.at[to], att_ss, att_rs, "batch", to, to).wait_recv()

    everyone = jnp.concatenate([att_all[b].astype(f32) for b in range(nb)], axis=0)
    projected = jnp.dot(everyone.astype(jnp.bfloat16), w_ref[...], preferred_element_type=f32)
    lines = out_ref.shape[0]
    for s in range(n):
        proj_send[s] = projected[s * lines : (s + 1) * lines].astype(proj_send.dtype)
    for i in range(1, n):
        to = lax.rem(me + i, n)
        push(proj_send.at[to], proj_recv.at[me], proj_ss, proj_rs, "seq", me, to).start()
    result = proj_send[me].astype(f32)
    for i in range(1, n):
        to = lax.rem(me + i, n)
        push(proj_send.at[to], proj_recv.at[to], proj_ss, proj_rs, "seq", to, to).wait_recv()
        result = result + proj_recv[to].astype(f32)
    out_ref[...] = result.astype(out_ref.dtype)

    for i in range(1, n):
        to = lax.rem(me + i, n)
        push(q_hbm, q_all.at[me], q_ss, q_rs, "seq", me, to).wait_send()
        push(stat_send.at[to], stat_recv.at[me], stat_ss, stat_rs, "seq", me, to).wait_send()
        push(sum_send.at[to], sum_recv.at[me], sum_ss, sum_rs, "seq", me, to).wait_send()
        push(proj_send.at[to], proj_recv.at[me], proj_ss, proj_rs, "seq", me, to).wait_send()
    for i in range(1, nb):
        to = lax.rem(mine + i, nb)
        push(att_all.at[mine], att_all.at[mine], att_ss, att_rs, "batch", mine, to).wait_send()


def on_device(n, nb, *args):
    queries, key_cache, value_cache, new_key, new_value, table, counts, offsets, w_out = args
    requests = queries.shape[0]
    own = HEADS // n
    lines = requests * nb // n
    columns = w_out.shape[1]
    bf16, f32 = jnp.bfloat16, jnp.float32
    hbm = pl.BlockSpec(memory_space=pl.ANY)
    smem = pl.BlockSpec(memory_space=pltpu.SMEM)
    dma = pltpu.SemaphoreType.DMA
    return pl.pallas_call(
        functools.partial(kernel, n, nb),
        out_shape=pltpu.VMEM((lines, columns), bf16),
        in_specs=[hbm] * 5 + [smem] * 3 + [hbm],
        out_specs=pl.BlockSpec(memory_space=pltpu.VMEM),
        scratch_shapes=[
            pltpu.VMEM((n,) + queries.shape, bf16),
            pltpu.VMEM(key_cache.shape, bf16),
            pltpu.VMEM(value_cache.shape, bf16),
            pltpu.VMEM(new_key.shape, bf16),
            pltpu.VMEM(new_value.shape, bf16),
            pltpu.VMEM(w_out.shape, bf16),
            pltpu.VMEM((n, 2, HD), f32),
            pltpu.VMEM((n, 2, HD), f32),
            pltpu.VMEM((n, own * requests, HD), f32),
            pltpu.VMEM((n, own * requests, HD), f32),
            pltpu.VMEM((nb,) + queries.shape, bf16),
            pltpu.VMEM((n, lines, columns), f32),
            pltpu.VMEM((n, lines, columns), f32),
            dma((6,)),
            dma((n,)),
            dma((n,)),
            dma((n,)),
            dma((n,)),
            dma((n,)),
            dma((n,)),
            dma((nb,)),
            dma((nb,)),
            dma((n,)),
            dma((n,)),
        ],
        compiler_params=pltpu.CompilerParams(collective_id=0, has_side_effects=True),
    )(*args[:5], table.T, counts.T, offsets, w_out)


def solution(mesh):
    placed = (
        P("batch", "seq"),
        P("batch", "seq", None),
        P("batch", "seq", None),
        P("batch", None),
        P("batch", None),
        P("batch", "seq"),
        P("batch", "seq"),
        P("batch"),
        P("seq", "batch"),
    )
    return jax.shard_map(
        functools.partial(on_device, mesh.shape["seq"], mesh.shape["batch"]),
        mesh=mesh,
        in_specs=placed,
        out_specs=P("seq", "batch"),
        check_vma=False,
    )
```

```python
import functools

import jax
import jax.numpy as jnp
from jax import lax
from jax.experimental import pallas as pl
from jax.experimental.pallas import tpu as pltpu
from jax.sharding import PartitionSpec as P

HEADS = 32
KVH = 16
HD = 128
QSCALAR = 144
CHUNK = 2

floor_score = -1e30


def kernel(
    n,
    nb,
    q_hbm,
    k_hbm,
    v_hbm,
    nk_hbm,
    nv_hbm,
    table_hbm,
    counts_hbm,
    offsets_hbm,
    w_hbm,
    out_ref,
    q_all,
    k_ref,
    v_ref,
    nk_ref,
    nv_ref,
    w_ref,
    table,
    counts,
    offsets,
    stat_send,
    stat_recv,
    sum_send,
    sum_recv,
    att_all,
    proj_send,
    proj_recv,
    load_sem,
    q_ss,
    q_rs,
    stat_ss,
    stat_rs,
    sum_ss,
    sum_rs,
    att_ss,
    att_rs,
    proj_ss,
    proj_rs,
):
    me = lax.axis_index("seq")
    mine = lax.axis_index("batch")
    requests = q_hbm.shape[0]
    slots, page_len, _ = k_hbm.shape
    pages = table_hbm.shape[0]
    tokens = slots * page_len
    groups = HEADS // KVH
    own = HEADS // n
    width = CHUNK * HD
    chunk_heads = CHUNK * groups
    rows = chunk_heads * requests
    n_chunks = KVH // CHUNK
    scale = QSCALAR ** (-0.5)
    f32 = jnp.float32

    loads = [
        pltpu.make_async_copy(src, dst, load_sem.at[i])
        for i, (src, dst) in enumerate(
            (
                (q_hbm, q_all.at[me]),
                (k_hbm, k_ref),
                (v_hbm, v_ref),
                (table_hbm, table),
                (counts_hbm, counts),
                (offsets_hbm, offsets),
                (nk_hbm, nk_ref),
                (nv_hbm, nv_ref),
                (w_hbm, w_ref),
            )
        )
    ]
    for load in loads:
        load.start()

    def partner(place, m):
        to, bit = place, 1
        while bit <= m:
            if m & bit:
                to = to + bit * (1 - 2 * ((place // bit) % 2))
            bit *= 2
        return to

    far_first = [partner(me, m) for m in range(n - 1, 0, -1)]
    near_first = far_first[::-1]
    far_batch = [partner(mine, m) for m in range(nb - 1, 0, -1)]

    barrier = pltpu.get_barrier_semaphore()
    for to in far_batch:
        pl.semaphore_signal(barrier, inc=1, device_id={"batch": to})
    for to in far_first:
        pl.semaphore_signal(barrier, inc=1, device_id={"seq": to})
    loads[0].wait()
    pl.semaphore_wait(barrier, n - 1 + nb - 1)

    def push(src, dst, ss, rs, axis, place, to):
        return pltpu.make_async_remote_copy(
            src_ref=src,
            dst_ref=dst,
            send_sem=ss.at[to],
            recv_sem=rs.at[place],
            device_id={axis: to},
        )

    def push_q(place, to):
        return push(q_all.at[me], q_all.at[place], q_ss, q_rs, "seq", place, to)

    def push_stat(place, to):
        return push(stat_send.at[to], stat_recv.at[place], stat_ss, stat_rs, "seq", place, to)

    def push_sum(place, to):
        return push(sum_send.at[to], sum_recv.at[place], sum_ss, sum_rs, "seq", place, to)

    def push_att(place, to):
        return push(att_all.at[mine], att_all.at[place], att_ss, att_rs, "batch", place, to)

    def push_proj(place, to):
        return push(proj_send.at[to], proj_recv.at[place], proj_ss, proj_rs, "seq", place, to)

    for to in far_first:
        push_q(me, to).start()
    for load in loads[1:6]:
        load.wait()

    row_request = lax.broadcasted_iota(jnp.int32, (rows, tokens), 0) % requests
    column = lax.broadcasted_iota(jnp.int32, (rows, tokens), 1)
    slot, token = column // page_len, column % page_len
    live = jnp.zeros((rows, tokens), jnp.bool_)
    first = jnp.zeros((rows, tokens), jnp.int32)
    for r in range(requests):
        first = jnp.where(row_request == r, offsets[0, r], first)
    for p in range(pages):
        where_at = jnp.zeros((rows, tokens), jnp.int32)
        count = jnp.zeros((rows, tokens), jnp.int32)
        for r in range(requests):
            where_at = jnp.where(row_request == r, table[p, r], where_at)
            count = jnp.where(row_request == r, counts[p, r], count)
        start = (me * pages + p) * page_len
        live = live | ((where_at == slot) & (token < count) & (start + token >= first))

    row = lax.broadcasted_iota(jnp.int32, (rows, HD), 0)
    lane = lax.broadcasted_iota(jnp.int32, (rows, HD), 1)

    def head_rows(ref, lead, head):
        at = pl.ds(pl.multiple_of(head * HD, HD), HD)
        return (ref[lead, :, at] if lead is not None else ref[:, at]).astype(f32)

    base = (me * own) // chunk_heads
    span = min(own, chunk_heads)
    per_chunk = chunk_heads // span
    half = groups * requests

    def unless_mine(step, to, run):
        if step:
            run()
        elif per_chunk > 1:
            pl.when(to != me)(run)

    def scores_of(c):
        at = pl.ds(pl.multiple_of(c * width, width), width)
        head0 = c * chunk_heads
        parts = []
        for h in range(chunk_heads):
            parts.append(head_rows(q_all, (head0 + h) // own, (head0 + h) % own))
        q = jnp.concatenate(parts, axis=0)
        wide = jnp.concatenate(
            [jnp.where(row // half == k, q, 0.0).astype(jnp.bfloat16) for k in range(CHUNK)],
            axis=1,
        )
        keys = k_ref[:, :, at].reshape(tokens, width)
        return lax.dot_general(wide, keys, (((1,), (1,)), ((), ())), preferred_element_type=f32)

    def softmax_of(scores):
        scores = scores * scale
        peak = jnp.max(jnp.where(live, scores, floor_score), axis=1, keepdims=True)
        weights = jnp.where(live, jnp.exp(scores - peak), 0.0)
        return peak, jnp.sum(weights, axis=1, keepdims=True), weights.astype(jnp.bfloat16)

    def sums_of(c, weights):
        at = pl.ds(pl.multiple_of(c * width, width), width)
        values = v_ref[:, :, at].reshape(tokens, width)
        full = jnp.dot(weights, values, preferred_element_type=f32)
        return jnp.concatenate(
            [full[k * half : (k + 1) * half, k * HD : (k + 1) * HD] for k in range(CHUNK)], axis=0
        )

    near = [m for m in range(2, n_chunks) if m < n_chunks - n_chunks // 4]
    far = [m for m in range(2, n_chunks) if m not in near]
    for steps in ([0], [1], near, far):
        chunks = [partner(base, m) for m in steps]
        for m, c in zip(steps, chunks):
            for part in range(per_chunk):
                src = c * per_chunk + part
                unless_mine(m, src, lambda src=src: push_q(src, src).wait_recv())
        scores = [scores_of(c) for c in chunks]
        soft = [softmax_of(x) for x in scores]
        sums = [sums_of(c, x[2]) for c, x in zip(chunks, soft)]
        height = span * requests
        for m, c, (peak, total, _), done in zip(steps, chunks, soft, sums):
            for part in range(per_chunk):
                to = c * per_chunk + part
                low = part * height
                hit = (row - low == lane) & (row >= low) & (row < low + height)
                stat_send[to] = jnp.concatenate(
                    [
                        jnp.sum(jnp.where(hit, peak, 0.0), axis=0, keepdims=True),
                        jnp.sum(jnp.where(hit, total, 0.0), axis=0, keepdims=True),
                    ],
                    axis=0,
                )
                sum_send[to] = done[low : low + height].astype(sum_send.dtype)
        for m, c in zip(steps, chunks):
            for part in range(per_chunk):
                to = c * per_chunk + part

                def send(to=to):
                    push_sum(me, to).start()
                    push_stat(me, to).start()

                unless_mine(m, to, send)

    own_rows = own * requests
    for load in loads[6:]:
        load.wait()
    kv = [(me * own + h) // groups for h in range(own)]
    own_q = jnp.concatenate([head_rows(q_all, me, h) for h in range(own)], axis=0)
    own_key = jnp.concatenate([head_rows(nk_ref, None, k) for k in kv], axis=0)
    own_value = jnp.concatenate([head_rows(nv_ref, None, k) for k in kv], axis=0)
    new_score = jnp.sum(own_q * own_key, axis=1, keepdims=True) * scale

    o_row = lax.broadcasted_iota(jnp.int32, (own_rows, HD), 0)
    o_lane = lax.broadcasted_iota(jnp.int32, (own_rows, HD), 1)
    diagonal = o_row == o_lane

    def to_column(line):
        return jnp.sum(jnp.where(diagonal, line, 0.0), axis=1, keepdims=True)

    for to in near_first:
        push_stat(to, to).wait_recv()
    stats = [stat_send[me]] + [stat_recv[to] for to in near_first]
    peaks = [to_column(s[0:1]) for s in stats]
    totals = [to_column(s[1:2]) for s in stats]
    top = new_score
    for peak in peaks:
        top = jnp.maximum(top, peak)
    own_weight = jnp.exp(new_score - top)
    factors = [jnp.exp(peak - top) for peak in peaks]
    denominator = own_weight
    for total, factor in zip(totals, factors):
        denominator = denominator + total * factor
    numerator = own_weight * own_value + factors[0] * sum_send[me].astype(f32)
    for to, factor in zip(near_first, factors[1:]):
        push_sum(to, to).wait_recv()
        numerator = numerator + factor * sum_recv[to].astype(f32)
    attention = numerator / denominator
    for h in range(own):
        att_all[mine, :, h * HD : (h + 1) * HD] = attention[
            h * requests : (h + 1) * requests
        ].astype(jnp.bfloat16)
    for to in far_batch:
        push_att(mine, to).start()
    for to in far_batch:
        push_att(to, to).wait_recv()

    everyone = jnp.concatenate([att_all[b].astype(f32) for b in range(nb)], axis=0)
    projected = jnp.dot(everyone.astype(jnp.bfloat16), w_ref[...], preferred_element_type=f32)
    lines = out_ref.shape[0]
    for s in range(n):
        proj_send[s] = projected[s * lines : (s + 1) * lines].astype(proj_send.dtype)
    for to in far_first:
        push_proj(me, to).start()
    result = proj_send[me].astype(f32)
    for to in near_first:
        push_proj(to, to).wait_recv()
        result = result + proj_recv[to].astype(f32)
    out_ref[...] = result.astype(out_ref.dtype)

    for to in far_first:
        for sent in (push_q, push_stat, push_sum, push_proj):
            sent(me, to).wait_send()
    for to in far_batch:
        push_att(mine, to).wait_send()


def on_device(n, nb, *args):
    queries, key_cache, value_cache, new_key, new_value, table, counts, offsets, w_out = args
    requests = queries.shape[0]
    own = HEADS // n
    lines = requests * nb // n
    columns = w_out.shape[1]
    bf16, f32 = jnp.bfloat16, jnp.float32
    hbm = pl.BlockSpec(memory_space=pl.ANY)
    dma = pltpu.SemaphoreType.DMA
    return pl.pallas_call(
        functools.partial(kernel, n, nb),
        out_shape=pltpu.VMEM((lines, columns), bf16),
        in_specs=[hbm] * 9,
        out_specs=pl.BlockSpec(memory_space=pltpu.VMEM),
        scratch_shapes=[
            pltpu.VMEM((n,) + queries.shape, bf16),
            pltpu.VMEM(key_cache.shape, bf16),
            pltpu.VMEM(value_cache.shape, bf16),
            pltpu.VMEM(new_key.shape, bf16),
            pltpu.VMEM(new_value.shape, bf16),
            pltpu.VMEM(w_out.shape, bf16),
            pltpu.SMEM(table.T.shape, jnp.int32),
            pltpu.SMEM(counts.T.shape, jnp.int32),
            pltpu.SMEM((1,) + offsets.shape, jnp.int32),
            pltpu.VMEM((n, 2, HD), f32),
            pltpu.VMEM((n, 2, HD), f32),
            pltpu.VMEM((n, own * requests, HD), bf16),
            pltpu.VMEM((n, own * requests, HD), bf16),
            pltpu.VMEM((nb,) + queries.shape, bf16),
            pltpu.VMEM((n, lines, columns), bf16),
            pltpu.VMEM((n, lines, columns), bf16),
            dma((9,)),
            dma((n,)),
            dma((n,)),
            dma((n,)),
            dma((n,)),
            dma((n,)),
            dma((n,)),
            dma((nb,)),
            dma((nb,)),
            dma((n,)),
            dma((n,)),
        ],
        compiler_params=pltpu.CompilerParams(collective_id=0, has_side_effects=True),
    )(*args[:5], table.T, counts.T, offsets[None], w_out)


def solution(mesh):
    placed = (
        P("batch", "seq"),
        P("batch", "seq", None),
        P("batch", "seq", None),
        P("batch", None),
        P("batch", None),
        P("batch", "seq"),
        P("batch", "seq"),
        P("batch"),
        P("seq", "batch"),
    )
    return jax.shard_map(
        functools.partial(on_device, mesh.shape["seq"], mesh.shape["batch"]),
        mesh=mesh,
        in_specs=placed,
        out_specs=P("seq", "batch"),
        check_vma=False,
    )
```

```python
import functools

import jax
import jax.numpy as jnp
from jax import lax
from jax.experimental import pallas as pl
from jax.experimental.pallas import tpu as pltpu
from jax.sharding import PartitionSpec as P

HEADS = 32
KVH = 16
HD = 128
QSCALAR = 144
CHUNK = 2

floor_score = -1e30


def kernel(
    n,
    nb,
    q_hbm,
    k_hbm,
    v_hbm,
    nk_hbm,
    nv_hbm,
    table_hbm,
    counts_hbm,
    offsets_hbm,
    w_hbm,
    out_ref,
    q_all,
    pools,
    fresh,
    w_ref,
    small,
    offsets,
    stat_send,
    stat_recv,
    sum_send,
    sum_recv,
    att_all,
    proj_send,
    proj_recv,
    load_sem,
    send_sem,
    recv_sem,
    q_rs,
):
    me = lax.axis_index("seq")
    mine = lax.axis_index("batch")
    requests = q_hbm.shape[0]
    slots, page_len, _ = k_hbm.shape
    pages = table_hbm.shape[0]
    tokens = slots * page_len
    groups = HEADS // KVH
    own = HEADS // n
    width = CHUNK * HD
    chunk_heads = CHUNK * groups
    rows = chunk_heads * requests
    n_chunks = KVH // CHUNK
    scale = QSCALAR ** (-0.5)
    f32 = jnp.float32

    def load(sources, held, sem):
        for i, src in enumerate(sources):
            pltpu.make_async_copy(src, held.at[i], load_sem.at[sem]).start()

        def wait():
            pltpu.make_async_copy(held, held, load_sem.at[sem]).wait()

        return wait

    q_load = pltpu.make_async_copy(q_hbm, q_all.at[me], load_sem.at[0])
    q_load.start()
    wait_pages = load((k_hbm, v_hbm), pools, 1)
    wait_small = load((table_hbm, counts_hbm), small, 2)
    offsets_load = pltpu.make_async_copy(offsets_hbm, offsets, load_sem.at[3])
    offsets_load.start()
    wait_new = load((nk_hbm, nv_hbm), fresh, 4)
    w_load = pltpu.make_async_copy(w_hbm, w_ref, load_sem.at[5])
    w_load.start()
    k_ref, v_ref = pools.at[0], pools.at[1]
    nk_ref, nv_ref = fresh.at[0], fresh.at[1]
    table, counts = small.at[0], small.at[1]

    def partner(place, m):
        to, bit = place, 1
        while bit <= m:
            if m & bit:
                to = to + bit * (1 - 2 * ((place // bit) % 2))
            bit *= 2
        return to

    far_first = [partner(me, m) for m in range(n - 1, 0, -1)]
    near_first = far_first[::-1]
    far_batch = [partner(mine, m) for m in range(nb - 1, 0, -1)]

    barrier = pltpu.get_barrier_semaphore()
    for to in far_batch:
        pl.semaphore_signal(barrier, inc=1, device_id={"batch": to})
    for to in far_first:
        pl.semaphore_signal(barrier, inc=1, device_id={"seq": to})
    q_load.wait()
    pl.semaphore_wait(barrier, n - 1 + nb - 1)

    def push(src, dst, ss, rs, axis, to):
        return pltpu.make_async_remote_copy(
            src_ref=src, dst_ref=dst, send_sem=ss, recv_sem=rs, device_id={axis: to}
        )

    def wait_bytes(buffer, parts, sem):
        if parts:
            some = buffer.at[pl.ds(0, parts)]
            pltpu.make_async_copy(some, some, sem).wait()

    def push_q(to, step):
        push(q_all.at[me], q_all.at[me], send_sem.at[0], q_rs.at[min(step, 2)], "seq", to).start()

    def push_stat(to):
        push(stat_send.at[to], stat_recv.at[me], send_sem.at[1], recv_sem.at[0], "seq", to).start()

    def push_sum(to):
        push(sum_send.at[to], sum_recv.at[me], send_sem.at[2], recv_sem.at[1], "seq", to).start()

    def push_att(to):
        mine_at = att_all.at[mine]
        push(mine_at, mine_at, send_sem.at[3], recv_sem.at[2], "batch", to).start()

    def push_proj(to):
        push(proj_send.at[to], proj_recv.at[me], send_sem.at[4], recv_sem.at[3], "seq", to).start()

    base = (me * own) // chunk_heads
    span = min(own, chunk_heads)
    per_chunk = chunk_heads // span
    half = groups * requests
    for m in range(n - 1, 0, -1):
        push_q(partner(me, m), m // per_chunk)
    wait_small()
    offsets_load.wait()

    row_request = lax.broadcasted_iota(jnp.int32, (rows, tokens), 0) % requests
    column = lax.broadcasted_iota(jnp.int32, (rows, tokens), 1)
    slot, token = column // page_len, column % page_len
    live = jnp.zeros((rows, tokens), jnp.bool_)
    first = jnp.zeros((rows, tokens), jnp.int32)
    for r in range(requests):
        first = jnp.where(row_request == r, offsets[0, r], first)
    for p in range(pages):
        where_at = jnp.zeros((rows, tokens), jnp.int32)
        count = jnp.zeros((rows, tokens), jnp.int32)
        for r in range(requests):
            where_at = jnp.where(row_request == r, table[p, r], where_at)
            count = jnp.where(row_request == r, counts[p, r], count)
        start = (me * pages + p) * page_len
        live = live | ((where_at == slot) & (token < count) & (start + token >= first))

    row = lax.broadcasted_iota(jnp.int32, (rows, HD), 0)
    lane = lax.broadcasted_iota(jnp.int32, (rows, HD), 1)

    def head_rows(ref, lead, head):
        at = pl.ds(pl.multiple_of(head * HD, HD), HD)
        return (ref[lead, :, at] if lead is not None else ref[:, at]).astype(f32)

    own_rows = own * requests
    wait_new()
    kv = [(me * own + h) // groups for h in range(own)]
    own_q = jnp.concatenate([head_rows(q_all, me, h) for h in range(own)], axis=0)
    own_key = jnp.concatenate([head_rows(nk_ref, None, k) for k in kv], axis=0)
    own_value = jnp.concatenate([head_rows(nv_ref, None, k) for k in kv], axis=0)
    new_score = jnp.sum(own_q * own_key, axis=1, keepdims=True) * scale

    wait_pages()

    def unless_mine(step, to, run):
        if step:
            run()
        elif per_chunk > 1:
            pl.when(to != me)(run)

    def scores_of(c):
        at = pl.ds(pl.multiple_of(c * width, width), width)
        head0 = c * chunk_heads
        parts = []
        for h in range(chunk_heads):
            parts.append(head_rows(q_all, (head0 + h) // own, (head0 + h) % own))
        q = jnp.concatenate(parts, axis=0)
        wide = jnp.concatenate(
            [jnp.where(row // half == k, q, 0.0).astype(jnp.bfloat16) for k in range(CHUNK)],
            axis=1,
        )
        keys = k_ref[:, :, at].reshape(tokens, width)
        return lax.dot_general(wide, keys, (((1,), (1,)), ((), ())), preferred_element_type=f32)

    def softmax_of(scores):
        scores = scores * scale
        peak = jnp.max(jnp.where(live, scores, floor_score), axis=1, keepdims=True)
        weights = jnp.where(live, jnp.exp(scores - peak), 0.0)
        return peak, jnp.sum(weights, axis=1, keepdims=True), weights.astype(jnp.bfloat16)

    def sums_of(c, weights):
        at = pl.ds(pl.multiple_of(c * width, width), width)
        values = v_ref[:, :, at].reshape(tokens, width)
        full = jnp.dot(weights, values, preferred_element_type=f32)
        return jnp.concatenate(
            [full[k * half : (k + 1) * half, k * HD : (k + 1) * HD] for k in range(CHUNK)], axis=0
        )

    for steps in ([0], [1], list(range(n_chunks - 1, 1, -1))):
        chunks = [partner(base, m) for m in steps]
        wait_bytes(q_all, per_chunk * len(steps) - (0 in steps), q_rs.at[min(steps[-1], 2)])
        scores = [scores_of(c) for c in chunks]
        soft = [softmax_of(x) for x in scores]
        sums = [sums_of(c, x[2]) for c, x in zip(chunks, soft)]
        height = span * requests
        for m, c, (peak, total, _), done in zip(steps, chunks, soft, sums):
            for part in range(per_chunk):
                to = c * per_chunk + part
                low = part * height
                hit = (row - low == lane) & (row >= low) & (row < low + height)
                stat_send[to] = jnp.concatenate(
                    [
                        jnp.sum(jnp.where(hit, peak, 0.0), axis=0, keepdims=True),
                        jnp.sum(jnp.where(hit, total, 0.0), axis=0, keepdims=True),
                    ],
                    axis=0,
                )
                sum_send[to] = done[low : low + height].astype(sum_send.dtype)
        for m, c in zip(steps, chunks):
            for part in range(per_chunk):
                to = c * per_chunk + part

                def send(to=to):
                    push_sum(to)
                    push_stat(to)

                unless_mine(m, to, send)

    o_row = lax.broadcasted_iota(jnp.int32, (own_rows, HD), 0)
    o_lane = lax.broadcasted_iota(jnp.int32, (own_rows, HD), 1)
    diagonal = o_row == o_lane

    def to_column(line):
        return jnp.sum(jnp.where(diagonal, line, 0.0), axis=1, keepdims=True)

    wait_bytes(stat_recv, n - 1, recv_sem.at[0])
    stats = [stat_send[me]] + [stat_recv[to] for to in near_first]
    peaks = [to_column(s[0:1]) for s in stats]
    totals = [to_column(s[1:2]) for s in stats]
    top = new_score
    for peak in peaks:
        top = jnp.maximum(top, peak)
    own_weight = jnp.exp(new_score - top)
    factors = [jnp.exp(peak - top) for peak in peaks]
    denominator = own_weight
    for total, factor in zip(totals, factors):
        denominator = denominator + total * factor
    numerator = own_weight * own_value + factors[0] * sum_send[me].astype(f32)
    wait_bytes(sum_recv, n - 1, recv_sem.at[1])
    for to, factor in zip(near_first, factors[1:]):
        numerator = numerator + factor * sum_recv[to].astype(f32)
    attention = numerator / denominator
    for h in range(own):
        att_all[mine, :, h * HD : (h + 1) * HD] = attention[
            h * requests : (h + 1) * requests
        ].astype(jnp.bfloat16)
    for to in far_batch:
        push_att(to)
    w_load.wait()
    wait_bytes(att_all, nb - 1, recv_sem.at[2])

    everyone = jnp.concatenate([att_all[b].astype(f32) for b in range(nb)], axis=0)
    projected = jnp.dot(everyone.astype(jnp.bfloat16), w_ref[...], preferred_element_type=f32)
    lines = out_ref.shape[0]
    for s in range(n):
        proj_send[s] = projected[s * lines : (s + 1) * lines].astype(proj_send.dtype)
    for to in far_first:
        push_proj(to)
    result = proj_send[me].astype(f32)
    wait_bytes(proj_recv, n - 1, recv_sem.at[3])
    for to in near_first:
        result = result + proj_recv[to].astype(f32)
    out_ref[...] = result.astype(out_ref.dtype)

    wait_bytes(q_all, n - 1, send_sem.at[0])
    wait_bytes(stat_send, n - 1, send_sem.at[1])
    wait_bytes(sum_send, n - 1, send_sem.at[2])
    wait_bytes(att_all, nb - 1, send_sem.at[3])
    wait_bytes(proj_send, n - 1, send_sem.at[4])


def on_device(n, nb, *args):
    queries, key_cache, value_cache, new_key, new_value, table, counts, offsets, w_out = args
    requests = queries.shape[0]
    own = HEADS // n
    lines = requests * nb // n
    columns = w_out.shape[1]
    bf16, f32 = jnp.bfloat16, jnp.float32
    hbm = pl.BlockSpec(memory_space=pl.ANY)
    dma = pltpu.SemaphoreType.DMA
    return pl.pallas_call(
        functools.partial(kernel, n, nb),
        out_shape=pltpu.VMEM((lines, columns), bf16),
        in_specs=[hbm] * 9,
        out_specs=pl.BlockSpec(memory_space=pltpu.VMEM),
        scratch_shapes=[
            pltpu.VMEM((n,) + queries.shape, bf16),
            pltpu.VMEM((2,) + key_cache.shape, bf16),
            pltpu.VMEM((2,) + new_key.shape, bf16),
            pltpu.VMEM(w_out.shape, bf16),
            pltpu.SMEM((2,) + table.T.shape, jnp.int32),
            pltpu.SMEM((1,) + offsets.shape, jnp.int32),
            pltpu.VMEM((n, 2, HD), f32),
            pltpu.VMEM((n, 2, HD), f32),
            pltpu.VMEM((n, own * requests, HD), bf16),
            pltpu.VMEM((n, own * requests, HD), bf16),
            pltpu.VMEM((nb,) + queries.shape, bf16),
            pltpu.VMEM((n, lines, columns), f32),
            pltpu.VMEM((n, lines, columns), f32),
            dma((6,)),
            dma((5,)),
            dma((4,)),
            dma((3,)),
        ],
        compiler_params=pltpu.CompilerParams(collective_id=0, has_side_effects=True),
    )(*args[:5], table.T, counts.T, offsets[None], w_out)


def solution(mesh):
    placed = (
        P("batch", "seq"),
        P("batch", "seq", None),
        P("batch", "seq", None),
        P("batch", None),
        P("batch", None),
        P("batch", "seq"),
        P("batch", "seq"),
        P("batch"),
        P("seq", "batch"),
    )
    return jax.shard_map(
        functools.partial(on_device, mesh.shape["seq"], mesh.shape["batch"]),
        mesh=mesh,
        in_specs=placed,
        out_specs=P("seq", "batch"),
        check_vma=False,
    )
```

```python
import functools

import jax
import jax.numpy as jnp
from jax import lax
from jax.experimental import pallas as pl
from jax.experimental.pallas import tpu as pltpu
from jax.sharding import PartitionSpec as P

HEADS = 32
KVH = 16
HD = 128
QSCALAR = 144
CHUNK = 2

floor_score = -1e30


def kernel(
    n,
    nb,
    q_hbm,
    k_hbm,
    v_hbm,
    nk_hbm,
    nv_hbm,
    table_hbm,
    counts_hbm,
    offsets_hbm,
    w_hbm,
    out_ref,
    q_all,
    pools,
    fresh,
    w_ref,
    small,
    offsets,
    stat_send,
    stat_recv,
    sum_send,
    sum_recv,
    att_all,
    proj_send,
    proj_recv,
    load_sem,
    send_sem,
    recv_sem,
    q_rs,
):
    me = lax.axis_index("seq")
    mine = lax.axis_index("batch")
    requests = q_hbm.shape[0]
    slots, page_len, _ = k_hbm.shape
    pages = table_hbm.shape[0]
    tokens = slots * page_len
    groups = HEADS // KVH
    own = HEADS // n
    width = CHUNK * HD
    chunk_heads = CHUNK * groups
    rows = chunk_heads * requests
    n_chunks = KVH // CHUNK
    scale = QSCALAR ** (-0.5)
    f32 = jnp.float32

    def load(sources, held, sem):
        for i, src in enumerate(sources):
            pltpu.make_async_copy(src, held.at[i], load_sem.at[sem]).start()

        def wait():
            pltpu.make_async_copy(held, held, load_sem.at[sem]).wait()

        return wait

    q_load = pltpu.make_async_copy(q_hbm, q_all.at[me], load_sem.at[0])
    q_load.start()
    wait_pages = load((k_hbm, v_hbm), pools, 1)
    wait_small = load((table_hbm, counts_hbm), small, 2)
    offsets_load = pltpu.make_async_copy(offsets_hbm, offsets, load_sem.at[3])
    offsets_load.start()
    wait_new = load((nk_hbm, nv_hbm), fresh, 4)
    w_load = pltpu.make_async_copy(w_hbm, w_ref, load_sem.at[5])
    w_load.start()
    k_ref, v_ref = pools.at[0], pools.at[1]
    nk_ref, nv_ref = fresh.at[0], fresh.at[1]
    table, counts = small.at[0], small.at[1]

    def partner(place, m):
        to, bit = place, 1
        while bit <= m:
            if m & bit:
                to = to + bit * (1 - 2 * ((place // bit) % 2))
            bit *= 2
        return to

    far_first = [partner(me, m) for m in range(n - 1, 0, -1)]
    near_first = far_first[::-1]
    far_batch = [partner(mine, m) for m in range(nb - 1, 0, -1)]

    barrier = pltpu.get_barrier_semaphore()
    for to in far_batch:
        pl.semaphore_signal(barrier, inc=1, device_id={"batch": to})
    for to in far_first:
        pl.semaphore_signal(barrier, inc=1, device_id={"seq": to})
    q_load.wait()
    pl.semaphore_wait(barrier, n - 1 + nb - 1)

    def push(src, dst, ss, rs, axis, to):
        return pltpu.make_async_remote_copy(
            src_ref=src, dst_ref=dst, send_sem=ss, recv_sem=rs, device_id={axis: to}
        )

    def wait_bytes(buffer, parts, sem):
        if parts:
            some = buffer.at[pl.ds(0, parts)]
            pltpu.make_async_copy(some, some, sem).wait()

    def push_q(to, step):
        push(q_all.at[me], q_all.at[me], send_sem.at[0], q_rs.at[min(step, 2)], "seq", to).start()

    def push_stat(to):
        push(stat_send.at[to], stat_recv.at[me], send_sem.at[1], recv_sem.at[0], "seq", to).start()

    def push_sum(to):
        push(sum_send.at[to], sum_recv.at[me], send_sem.at[2], recv_sem.at[1], "seq", to).start()

    def push_att(to):
        mine_at = att_all.at[mine]
        push(mine_at, mine_at, send_sem.at[3], recv_sem.at[2], "batch", to).start()

    def push_proj(to):
        push(proj_send.at[to], proj_recv.at[me], send_sem.at[4], recv_sem.at[3], "seq", to).start()

    base = (me * own) // chunk_heads
    span = min(own, chunk_heads)
    per_chunk = chunk_heads // span
    half = groups * requests
    for m in range(n - 1, 0, -1):
        push_q(partner(me, m), m // per_chunk)
    wait_small()
    offsets_load.wait()

    row_request = lax.broadcasted_iota(jnp.int32, (rows, tokens), 0) % requests
    column = lax.broadcasted_iota(jnp.int32, (rows, tokens), 1)
    slot, token = column // page_len, column % page_len
    live = jnp.zeros((rows, tokens), jnp.bool_)
    first = jnp.zeros((rows, tokens), jnp.int32)
    for r in range(requests):
        first = jnp.where(row_request == r, offsets[0, r], first)
    for p in range(pages):
        where_at = jnp.zeros((rows, tokens), jnp.int32)
        count = jnp.zeros((rows, tokens), jnp.int32)
        for r in range(requests):
            where_at = jnp.where(row_request == r, table[p, r], where_at)
            count = jnp.where(row_request == r, counts[p, r], count)
        start = (me * pages + p) * page_len
        live = live | ((where_at == slot) & (token < count) & (start + token >= first))

    row = lax.broadcasted_iota(jnp.int32, (rows, HD), 0)
    lane = lax.broadcasted_iota(jnp.int32, (rows, HD), 1)

    def head_rows(ref, lead, head):
        at = pl.ds(pl.multiple_of(head * HD, HD), HD)
        return (ref[lead, :, at] if lead is not None else ref[:, at]).astype(f32)

    own_rows = own * requests
    wait_new()
    kv = [(me * own + h) // groups for h in range(own)]
    own_q = jnp.concatenate([head_rows(q_all, me, h) for h in range(own)], axis=0)
    own_key = jnp.concatenate([head_rows(nk_ref, None, k) for k in kv], axis=0)
    own_value = jnp.concatenate([head_rows(nv_ref, None, k) for k in kv], axis=0)
    new_score = jnp.sum(own_q * own_key, axis=1, keepdims=True) * scale

    wait_pages()

    def unless_mine(step, to, run):
        if step:
            run()
        elif per_chunk > 1:
            pl.when(to != me)(run)

    def scores_of(c):
        at = pl.ds(pl.multiple_of(c * width, width), width)
        head0 = c * chunk_heads
        parts = []
        for h in range(chunk_heads):
            parts.append(head_rows(q_all, (head0 + h) // own, (head0 + h) % own))
        q = jnp.concatenate(parts, axis=0)
        wide = jnp.concatenate(
            [jnp.where(row // half == k, q, 0.0).astype(jnp.bfloat16) for k in range(CHUNK)],
            axis=1,
        )
        keys = k_ref[:, :, at].reshape(tokens, width)
        return lax.dot_general(wide, keys, (((1,), (1,)), ((), ())), preferred_element_type=f32)

    def softmax_of(scores):
        scores = scores * scale
        peak = jnp.max(jnp.where(live, scores, floor_score), axis=1, keepdims=True)
        weights = jnp.where(live, jnp.exp(scores - peak), 0.0)
        return peak, jnp.sum(weights, axis=1, keepdims=True), weights.astype(jnp.bfloat16)

    def sums_of(c, weights):
        at = pl.ds(pl.multiple_of(c * width, width), width)
        values = v_ref[:, :, at].reshape(tokens, width)
        full = jnp.dot(weights, values, preferred_element_type=f32)
        return jnp.concatenate(
            [full[k * half : (k + 1) * half, k * HD : (k + 1) * HD] for k in range(CHUNK)], axis=0
        )

    for steps in ([0], [1], list(range(n_chunks - 1, 1, -1))):
        chunks = [partner(base, m) for m in steps]
        wait_bytes(q_all, per_chunk * len(steps) - (0 in steps), q_rs.at[min(steps[-1], 2)])
        scores = [scores_of(c) for c in chunks]
        soft = [softmax_of(x) for x in scores]
        sums = [sums_of(c, x[2]) for c, x in zip(chunks, soft)]
        height = span * requests
        for m, c, (peak, total, _), done in zip(steps, chunks, soft, sums):
            for part in range(per_chunk):
                to = c * per_chunk + part
                low = part * height
                hit = (row - low == lane) & (row >= low) & (row < low + height)
                stat_send[to] = jnp.concatenate(
                    [
                        jnp.sum(jnp.where(hit, peak, 0.0), axis=0, keepdims=True),
                        jnp.sum(jnp.where(hit, total, 0.0), axis=0, keepdims=True),
                    ],
                    axis=0,
                )
                sum_send[to] = done[low : low + height].astype(sum_send.dtype)
        for m, c in zip(steps, chunks):
            for part in range(per_chunk):
                to = c * per_chunk + part

                def send(to=to):
                    push_sum(to)
                    push_stat(to)

                unless_mine(m, to, send)

    o_row = lax.broadcasted_iota(jnp.int32, (own_rows, HD), 0)
    o_lane = lax.broadcasted_iota(jnp.int32, (own_rows, HD), 1)
    diagonal = o_row == o_lane

    def to_column(line):
        return jnp.sum(jnp.where(diagonal, line, 0.0), axis=1, keepdims=True)

    wait_bytes(stat_recv, n - 1, recv_sem.at[0])
    stats = [stat_send[me]] + [stat_recv[to] for to in near_first]
    peaks = [to_column(s[0:1]) for s in stats]
    totals = [to_column(s[1:2]) for s in stats]
    top = new_score
    for peak in peaks:
        top = jnp.maximum(top, peak)
    own_weight = jnp.exp(new_score - top)
    factors = [jnp.exp(peak - top) for peak in peaks]
    denominator = own_weight
    for total, factor in zip(totals, factors):
        denominator = denominator + total * factor
    numerator = own_weight * own_value + factors[0] * sum_send[me].astype(f32)
    wait_bytes(sum_recv, n - 1, recv_sem.at[1])
    for to, factor in zip(near_first, factors[1:]):
        numerator = numerator + factor * sum_recv[to].astype(f32)
    attention = numerator / denominator
    for h in range(own):
        att_all[mine, :, h * HD : (h + 1) * HD] = attention[
            h * requests : (h + 1) * requests
        ].astype(jnp.bfloat16)
    for to in far_batch:
        push_att(to)
    w_load.wait()
    wait_bytes(att_all, nb - 1, recv_sem.at[2])

    everyone = jnp.concatenate([att_all[b].astype(f32) for b in range(nb)], axis=0)
    projected = jnp.dot(everyone.astype(jnp.bfloat16), w_ref[...], preferred_element_type=f32)
    lines = out_ref.shape[0]
    for s in range(n):
        proj_send[s] = projected[s * lines : (s + 1) * lines].astype(proj_send.dtype)
    for to in far_first:
        push_proj(to)
    result = proj_send[me].astype(f32)
    wait_bytes(proj_recv, n - 1, recv_sem.at[3])
    for to in near_first:
        result = result + proj_recv[to].astype(f32)
    out_ref[...] = result.astype(out_ref.dtype)

    wait_bytes(q_all, n - 1, send_sem.at[0])
    wait_bytes(stat_send, n - 1, send_sem.at[1])
    wait_bytes(sum_send, n - 1, send_sem.at[2])
    wait_bytes(att_all, nb - 1, send_sem.at[3])
    wait_bytes(proj_send, n - 1, send_sem.at[4])


def on_device(n, nb, *args):
    queries, key_cache, value_cache, new_key, new_value, table, counts, offsets, w_out = args
    requests = queries.shape[0]
    own = HEADS // n
    lines = requests * nb // n
    columns = w_out.shape[1]
    bf16, f32 = jnp.bfloat16, jnp.float32
    hbm = pl.BlockSpec(memory_space=pl.ANY)
    dma = pltpu.SemaphoreType.DMA
    return pl.pallas_call(
        functools.partial(kernel, n, nb),
        out_shape=pltpu.VMEM((lines, columns), bf16),
        in_specs=[hbm] * 9,
        out_specs=pl.BlockSpec(memory_space=pltpu.VMEM),
        scratch_shapes=[
            pltpu.VMEM((n,) + queries.shape, bf16),
            pltpu.VMEM((2,) + key_cache.shape, bf16),
            pltpu.VMEM((2,) + new_key.shape, bf16),
            pltpu.VMEM(w_out.shape, bf16),
            pltpu.SMEM((2,) + table.T.shape, jnp.int32),
            pltpu.SMEM((1,) + offsets.shape, jnp.int32),
            pltpu.VMEM((n, 2, HD), f32),
            pltpu.VMEM((n, 2, HD), f32),
            pltpu.VMEM((n, own * requests, HD), bf16),
            pltpu.VMEM((n, own * requests, HD), bf16),
            pltpu.VMEM((nb,) + queries.shape, bf16),
            pltpu.VMEM((n, lines, columns), bf16),
            pltpu.VMEM((n, lines, columns), bf16),
            dma((6,)),
            dma((5,)),
            dma((4,)),
            dma((3,)),
        ],
        compiler_params=pltpu.CompilerParams(collective_id=0, has_side_effects=True),
    )(*args[:5], table.T, counts.T, offsets[None], w_out)


def solution(mesh):
    placed = (
        P("batch", "seq"),
        P("batch", "seq", None),
        P("batch", "seq", None),
        P("batch", None),
        P("batch", None),
        P("batch", "seq"),
        P("batch", "seq"),
        P("batch"),
        P("seq", "batch"),
    )
    return jax.shard_map(
        functools.partial(on_device, mesh.shape["seq"], mesh.shape["batch"]),
        mesh=mesh,
        in_specs=placed,
        out_specs=P("seq", "batch"),
        check_vma=False,
    )
```
